32 devices in a mesh: groups: 2 (over x), lon: 8 (over z, y), lat: 2 (over core).
Axes of the slice: x: 2, y: 2, z: 4, core: 2. Of those that a mesh axis runs over, the one named last changes fastest.
Arguments:
- atmosphere: bfloat16 [256, 128, 512], P(('groups', 'lat'), 'lon'), parts along dimension 0, may hold values from -6 to 6
- pole_band: int32 [256], P(('groups', 'lat')), parts along dimension 0, may hold values from 0 to 15, never falling along the last dimension, each value on 1 to 96 neighbouring positions
- key_valid: int32 [256, 128], P(('groups', 'lat'), 'lon'), parts along dimension 0, may hold values 0 or 1
- norm_gains: float32 [2, 2, 512], replicated, may hold values from 0.5 to 1.5
- attend_in: bfloat16 [2, 512, 1536], replicated, as said below
- attend_out: bfloat16 [2, 512, 512], replicated, may hold values from -0.25 to 0.25
- expand: bfloat16 [2, 512, 1024], replicated, may hold values from -0.25 to 0.25
- contract: bfloat16 [2, 1024, 512], replicated, may hold values from -0.1875 to 0.1875
Outputs:
- evolved: bfloat16 [256, 128, 512], P(('groups', 'lat'), 'lon'), parts along dimension 0
The draws below stay inside these ranges and needn't reach their ends.
There are 2 independent parts, one for each index of `groups`. The reference program is written for one: setup_inputs(seed, part) draws one part's arguments, and reference() takes and returns one part's arrays. A program takes and returns all parts, laid end to end along the dimension named above; an argument that names none is the same for every part. Nothing has to cross between parts.
Inputs may be any that keep to these rules, and one draw needn't show every extreme that they name: `pole_band`: band numbers never fall along latitude, every number from 0 to the largest is used, and a band holds 1 to 96 rows. `attend_in`: query and value entries of order one over the square root of 512.
All inputs are finite; a program needn't handle non-finite values. No bound on the sum of `key_valid` on one device may be relied on, other than what follows from the above.
Results may differ from the reference program's by a relative error of at most 0.011.
Values may be sent and summed in bfloat16 or wider, within the bound.
A program may use at most 128 MiB of HBM per device.

```python
import math
import jax
import jax.numpy as jnp
import numpy as np
from jax import lax

D = 512
H = 8
FF = 1024
WH = 32
WW = 16
LAYERS = 2
HD = 64
SH = 16
SW = 8
LAT = 128
LON = 128


def draw_attend_in(key, part):
    base = jax.random.truncated_normal(key, -3.0, 3.0, (LAYERS, D, 3 * D), jnp.float32) / math.sqrt(D)
    return base.astype(jnp.bfloat16)


def place_ends(values, key, least, largest):
    longest = values.shape.index(max(values.shape))
    spots = []
    for shift in (0, 1):
        where = [jax.random.randint(jax.random.fold_in(key, axis), (), 0, length) for axis, length in enumerate(values.shape)]
        where[longest] = (where[longest] + shift) % values.shape[longest]
        spots.append(tuple(where))
    return values.at[spots[0]].set(least).at[spots[1]].set(largest)


def levels(rng, dims, shards, least, top_value):
    factor_of, own = 1.0, jax.random.fold_in(rng, 6)
    for axis_at, blocks in shards:
        steps = jnp.exp(jax.random.uniform(jax.random.fold_in(own, axis_at), (blocks,), jnp.float32, least / len(shards), top_value / len(shards)))
        factor_of = factor_of * jnp.repeat(steps, dims[axis_at] // blocks).reshape([-1 if axis == axis_at else 1 for axis in range(len(dims))])
    return factor_of


def profile(count, total, limit, lean):
    loads = [(1 << 20) // math.isqrt(rank ** lean) + 1 for rank in range(2, count + 1)]
    spare, given = total - limit - (count - 1), [1] * (count - 1)
    while spare > 0:
        movable = [i for i in range(count - 1) if given[i] < limit]
        whole, budget = sum([loads[i] for i in movable]), spare
        for i in movable:
            more = min(limit - given[i], max(1, budget * loads[i] // whole), spare)
            given[i] = given[i] + more
            spare = spare - more
    return np.array([limit] + given)


def ragged(stream_key, count, total, bound, skew):
    if count == 2:
        one = jax.random.randint(stream_key, (), max(1, total - bound), min(bound, total - 1) + 1)
        return jnp.stack([one, total - one])
    lengths = jnp.asarray(profile(count, total, bound, skew), jnp.int32)
    twos = (count - 1) // 2
    giver, sink = lengths[1:1 + 2 * twos:2], lengths[2:2 + 2 * twos:2]
    room = jnp.minimum(giver - 1, bound - sink)
    moved = jax.random.randint(jax.random.fold_in(stream_key, 1), (twos,), 0, 1 << 20) % (room + 1)
    lengths = lengths.at[1:1 + 2 * twos:2].set(giver - moved).at[2:2 + 2 * twos:2].set(sink + moved)
    return lengths[jax.random.permutation(jax.random.fold_in(stream_key, 2), count)]


def gaussian(stream_key, dims, scale, reach, pieces=(), held_as=jnp.bfloat16):
    loudness = levels(stream_key, dims, pieces, -0.22, 0.18) if pieces else 1.0
    drawn = jax.random.normal(stream_key, dims, jnp.float32) * scale * loudness
    return jnp.minimum(jnp.maximum(drawn, -reach), reach).astype(held_as)


def setup_inputs(seed: int = 0, part: int = 0) -> dict:
    streams_of = jax.random.split(jax.random.key(seed), 9)
    part_splits = jax.random.split(jax.random.fold_in(streams_of[8], part), 9)
    return {
        "atmosphere": gaussian(part_splits[0], (LAT, LON, D), 1.0, 6.0, ((0, 2), (1, 8))),
        "pole_band": jnp.searchsorted(jnp.cumsum(ragged(part_splits[1], max(2, LAT // 8), LAT, 3 * LAT // 4, 0)), jnp.arange(LAT), side="right").astype(jnp.int32),
        "key_valid": place_ends((jax.random.randint(part_splits[2], (LAT, LON), 0, 4) < 3).astype(jnp.int32), jax.random.fold_in(part_splits[2], 1), 0, 1),
        "norm_gains": jnp.clip(1.0 + 0.1 * jax.random.normal(streams_of[3], (LAYERS, 2, D), jnp.float32), 0.5, 1.5),
        "attend_in": draw_attend_in(jax.random.fold_in(streams_of[8], 71), part),
        "attend_out": gaussian(streams_of[5], (LAYERS, D, D), D ** -0.5, 0.25),
        "expand": gaussian(streams_of[6], (LAYERS, D, FF), D ** -0.5, 0.25),
        "contract": gaussian(streams_of[7], (LAYERS, FF, D), FF ** -0.5, 0.1875),
    }


norm_eps = 1e-05

def normalize(field, gains):
    widened = field.astype(jnp.float32)
    average = lax.optimization_barrier(jnp.mean(widened, -1, keepdims=True))
    centred = widened - average
    spread = lax.optimization_barrier(jnp.mean(centred * centred, -1, keepdims=True))
    return (centred * lax.rsqrt(spread + norm_eps) * gains).astype(jnp.bfloat16)

def windows_of(field):
    height, breadth = (field.shape[0], field.shape[1])
    rest = field.shape[2:]
    tiles = field.reshape((height // WH, WH, breadth // WW, WW) + rest)
    return jnp.swapaxes(tiles, 1, 2).reshape((-1, WH * WW) + rest)

def field_of(tiles, height, breadth):
    rest = tiles.shape[2:]
    grid = tiles.reshape((height // WH, breadth // WW, WH, WW) + rest)
    return jnp.swapaxes(grid, 1, 2).reshape((height, breadth) + rest)

def attend_window(packed, bands, masks):
    cells = packed.shape[0]
    heads = packed.reshape(cells, 3, H, HD).astype(jnp.float32)
    queries = heads[:, 0]
    keyed = heads[:, 1]
    valued = heads[:, 2]
    scores = jnp.einsum('qhd,khd->hqk', queries, keyed) * (1.0 / math.sqrt(HD))
    itself = jnp.arange(cells)[:, None] == jnp.arange(cells)[None, :]
    allowed = (bands[:, None] == bands[None, :]) & ((masks[None, :] == 1) | itself)
    scores = jnp.where(allowed[None], scores, -1e+30)
    row_max = lax.optimization_barrier(jnp.max(scores, -1, keepdims=True))
    raw_weights = jnp.exp(scores - row_max)
    probs = (raw_weights / lax.optimization_barrier(jnp.sum(raw_weights, -1, keepdims=True))).astype(jnp.bfloat16)
    context = jnp.einsum('hqk,khd->qhd', probs.astype(jnp.float32), valued)
    return context.astype(jnp.bfloat16).reshape(cells, D)

def layer(field, bands, masks, index, norm_gains, attend_in, attend_out, expand, contract):
    height, breadth = (field.shape[0], field.shape[1])
    normed = normalize(field, norm_gains[index, 0]).reshape(-1, D)
    projected = jnp.dot(normed, attend_in[index], preferred_element_type=jnp.float32)
    projected = projected.astype(jnp.bfloat16).reshape(height, breadth, 3 * D)
    band_grid = jnp.broadcast_to(bands[:, None], (height, breadth))
    context = lax.map(lambda item: attend_window(item[0], item[1], item[2]), (windows_of(projected), windows_of(band_grid), windows_of(masks)))
    context = field_of(context, height, breadth).reshape(-1, D)
    resid = field.reshape(-1, D).astype(jnp.float32) + jnp.dot(context, attend_out[index], preferred_element_type=jnp.float32)
    resid = resid.astype(jnp.bfloat16)
    normed_mlp = normalize(resid, norm_gains[index, 1])
    hidden = jax.nn.gelu(jnp.dot(normed_mlp, expand[index], preferred_element_type=jnp.float32), approximate=True)
    hidden = hidden.astype(jnp.bfloat16)
    layer_out = resid.astype(jnp.float32) + jnp.dot(hidden, contract[index], preferred_element_type=jnp.float32)
    return layer_out.astype(jnp.bfloat16).reshape(height, breadth, D)

def reference(atmosphere, pole_band, key_valid, norm_gains, attend_in, attend_out, expand, contract):
    shifted = jnp.roll(atmosphere, (-SH, -SW), axis=(0, 1))
    shifted_band = jnp.roll(pole_band, -SH)
    shifted_valid = jnp.roll(key_valid, (-SH, -SW), axis=(0, 1))
    first = layer(shifted, shifted_band, shifted_valid, 0, norm_gains, attend_in, attend_out, expand, contract)
    back = jnp.roll(first, (SH, SW), axis=(0, 1))
    return layer(back, pole_band, key_valid, 1, norm_gains, attend_in, attend_out, expand, contract)
```

```python
import functools
import math

import jax
import jax.numpy as jnp
from jax import lax
from jax.experimental import pallas as pl
from jax.experimental.pallas import tpu as pltpu
from jax.sharding import PartitionSpec as P

H = 8
WH = 32
SH = 16
SW = 8
EPS = 1e-05
MESH = pl.DeviceIdType.MESH
F32 = jnp.float32
BF16 = jnp.bfloat16


def norm(wide, gains):
    centred = wide - jnp.mean(wide, -1, keepdims=True)
    spread = jnp.mean(centred * centred, -1, keepdims=True)
    return (centred * lax.rsqrt(spread + EPS) * gains).astype(BF16)


def gelu(v):
    inner = v * (math.sqrt(2.0 / math.pi) + (math.sqrt(2.0 / math.pi) * 0.044715) * (v * v))
    half = 0.5 * v
    return half + half * jnp.tanh(inner)


def kernel(
    names, sizes, atm, band_in, valid_in, gains_in, w_in, w_out, w_up, w_down, out,
    xs, ys, code, cs, band, valid, gains, win, wout, wup, wdown, q2, ks, vs, bias, ctx,
    send, recv, local,
):
    height = atm.shape[0]
    width = atm.shape[2]
    count = height // WH
    cells = WH * SW
    pairs = width // 128
    body = height - SH
    last = height // SH - 1
    at = {name: lax.axis_index(name) for name in names}

    def device(lat, lon):
        spot = dict(at)
        spot["lat"] = lax.rem(at["lat"] + lat + sizes["lat"], sizes["lat"])
        spot["lon"] = lax.rem(at["lon"] + lon + sizes["lon"], sizes["lon"])
        return tuple(spot[name] for name in names)

    barrier = pltpu.get_barrier_semaphore()
    sources = ((1, 0), (0, -1), (1, -1))
    for lat, lon in sources:
        pl.semaphore_signal(barrier, inc=1, device_id=device(lat, lon), device_id_type=MESH)

    loads = []

    def load(src, dst):
        copy = pltpu.make_async_copy(src, dst, local.at[len(loads)])
        copy.start()
        loads.append(copy)
        return copy

    west, east = pl.ds(0, SW), pl.ds(SW, SW)
    small = [load(band_in, band), load(valid_in, valid), load(gains_in, gains)]
    own = load(atm.at[pl.ds(SH, body), west, :], xs.at[0, 0, pl.ds(0, body)])
    weights = {}
    for layer in range(2):
        for name, src, dst in (
            ("in", w_in, win), ("out", w_out, wout), ("up", w_up, wup), ("down", w_down, wdown),
        ):
            weights[name, layer] = load(src.at[layer], dst.at[layer])

    for copy in small:
        copy.wait()
    mixed = (2 * band[...] + valid[...]).astype(F32).astype(BF16)
    lane = lax.broadcasted_iota(jnp.int32, (mixed.shape[0], SH * SW), 1)
    column = lax.broadcasted_iota(jnp.int32, (mixed.shape[0], SH * SW), 0)
    lane_row = lax.broadcasted_iota(jnp.int32, (SH, SH * SW), 1) // SW
    keep = lane_row == lax.broadcasted_iota(jnp.int32, (SH, SH * SW), 0)
    for h in range(2):
        pick = jnp.where(column == lane % SW + SW * h, 1.0, 0.0).astype(BF16)
        spread = lax.dot_general(
            mixed, pick, (((0,), (0,)), ((), ())), preferred_element_type=F32)
        for chunk in range(last + 1):
            rows = jnp.where(keep, spread[SH * chunk:SH * chunk + SH], 0.0)
            rows = jnp.sum(rows, 0, keepdims=True).astype(jnp.int32)
            code[h, chunk] = jnp.broadcast_to(rows, (8, SH * SW))

    pl.semaphore_wait(barrier, len(sources))

    sent = []

    def push(src, dst, lat, lon):
        copy = pltpu.make_async_remote_copy(
            src_ref=src, dst_ref=dst, send_sem=send.at[len(sent)], recv_sem=recv.at[len(sent)],
            device_id=device(lat, lon), device_id_type=MESH,
        )
        copy.start()
        sent.append(copy)
        return copy

    got_code = [
        push(code.at[1, pl.ds(1, last)], cs.at[1, pl.ds(0, last)], 0, 1),
        push(code.at[0, pl.ds(0, 1)], cs.at[0, pl.ds(last, 1)], -1, 0),
        push(code.at[1, pl.ds(0, 1)], cs.at[1, pl.ds(last, 1)], -1, 1),
    ]
    got = []
    for w in range(count):
        rows = WH if w < count - 1 else WH - SH
        got.append([push(
            atm.at[pl.ds(SH + w * WH, rows), east, :], xs.at[0, 1, pl.ds(w * WH, rows)], 0, 1)])
    got_lat = push(atm.at[pl.ds(0, SH), west, :], xs.at[0, 0, pl.ds(body, SH)], -1, 0)

    vs[:, :, pl.ds(64, 16), :] = jnp.ones(vs.shape[:2] + (16, vs.shape[3]), BF16)
    low = lax.broadcasted_iota(jnp.int32, (cells, 128), 1) < 64
    scale = math.log2(math.e) / math.sqrt(64)

    def codes_of(layer, w):
        found = []
        for h in range(2):
            for chunk in (2 * w, 2 * w + 1):
                if layer == 1:
                    found.append(code[h, chunk])
                elif h == 0 and chunk < last:
                    found.append(code[0, chunk + 1])
                else:
                    found.append(cs[h, chunk])
        return found

    def make_bias(layer, w):
        found = codes_of(layer, w)
        across = jnp.concatenate(found, 1)[0:1]
        total = across.shape[1]
        band_across = jnp.broadcast_to(across >> 1, (128, total))
        row = lax.broadcasted_iota(jnp.int32, (128, total), 0)
        col = lax.broadcasted_iota(jnp.int32, (128, total), 1)
        for i, one in enumerate(found):
            down = jnp.broadcast_to(one[0:1].astype(F32), (128, 128)).T.astype(jnp.int32)
            down = jnp.concatenate([down] * (total // 128), 1)
            allowed = ((down >> 1) == band_across) & (((down & 1) == 1) | (row + 128 * i == col))
            bias[w, pl.ds(128 * i, 128), :] = jnp.where(allowed, 0.0, -1e30)

    def field(layer, w, h):
        return xs[layer, h, pl.ds(w * WH, WH)].astype(F32).reshape(cells, width)

    def project(layer, w, h):
        normed = norm(field(layer, w, h), gains[layer, 0:1, :])
        rows = pl.ds(h * cells, cells)
        for part in range(3):
            made = jnp.dot(
                normed, win[layer, :, pl.ds(part * width, width)], preferred_element_type=F32)
            if part == 2:
                turned = made.T.astype(BF16)
                for head in range(2 * pairs):
                    vs[w, head, pl.ds(0, 64), rows] = turned[64 * head:64 * head + 64]
                continue
            for p in range(pairs):
                two = made[:, 128 * p:128 * p + 128]
                if part == 0:
                    two = two * scale
                    q2[w, p, h, pl.ds(0, cells), :] = jnp.where(low, two, 0.0).astype(BF16)
                    q2[w, p, h, pl.ds(cells, cells), :] = jnp.where(low, 0.0, two).astype(BF16)
                else:
                    ks[w, p, rows, :] = two.astype(BF16)

    half_keys = cells

    def attend(layer, w, h, slot):
        heads = 2 * pairs
        scores = [[None, None] for _ in range(heads)]
        tops = [[None, None] for _ in range(heads)]

        def score(j, c):
            p, odd = j // 2, j % 2
            rows = pl.ds(half_keys * c, half_keys)
            made = lax.dot_general(
                ks[w, p, rows, :], q2[w, p, h, pl.ds(cells * odd, cells), :],
                (((1,), (1,)), ((), ())), preferred_element_type=F32)
            made = made + bias[w, rows, pl.ds(h * cells, cells)]
            scores[j][c] = made
            tops[j][c] = jnp.max(made, 0, keepdims=True)

        def weigh(j, c, top):
            raw = jnp.exp2(scores[j][c] - top).astype(BF16)
            scores[j][c] = None
            return jnp.dot(
                vs[w, j, :, pl.ds(half_keys * c, half_keys)], raw, preferred_element_type=F32)

        for j in range(heads + 1):
            made = None
            top = None if j == 0 else jnp.maximum(tops[j - 1][0], tops[j - 1][1])
            for c in range(2):
                if j < heads:
                    score(j, c)
                if j > 0:
                    part = weigh(j - 1, c, top)
                    made = part if made is None else made + part
            if j > 0:
                ctx[slot, pl.ds(64 * (j - 1), 64), :] = made[:64] / made[64:65]
            yield

    def finish(layer, w, h, slot, done):
        step = 256
        turned = ctx[slot].T.astype(BF16)
        own_field = field(layer, w, h)
        parts = []
        for n in range(0, width, step):
            parts.append(own_field[:, n:n + step] + jnp.dot(
                turned, wout[layer, :, pl.ds(n, step)], preferred_element_type=F32))
            yield
        resid = jnp.concatenate(parts, 1).astype(BF16).astype(F32)
        normed = norm(resid, gains[layer, 1:2, :])
        yield
        hidden = []
        for n in range(0, wup.shape[2], step):
            hidden.append(gelu(jnp.dot(
                normed, wup[layer, :, pl.ds(n, step)], preferred_element_type=F32)).astype(BF16))
            yield
        hidden = jnp.concatenate(hidden, 1)
        parts = []
        for n in range(0, width, step):
            parts.append(resid[:, n:n + step] + jnp.dot(
                hidden, wdown[layer, :, pl.ds(n, step)], preferred_element_type=F32))
            yield
        done(jnp.concatenate(parts, 1).reshape(WH, SW, width).astype(BF16))

    def together(*works):
        works = list(works)
        while works:
            for work in list(works):
                if next(work, works) is works:
                    works.remove(work)

    own.wait()
    weights["in", 0].wait()
    for w in range(count):
        if w == count - 1:
            got_lat.wait_recv()
        project(0, w, 0)
    for copy in got_code:
        copy.wait_recv()
    for w in range(count):
        make_bias(0, w)
    got[0][0].wait_send()
    got[count - 1].append(push(
        atm.at[pl.ds(0, SH), east, :], xs.at[0, 1, pl.ds(body, SH)], -1, 1))
    back = {}

    def send_west(w):
        rows = WH if w < count - 1 else WH - SH

        def done(made):
            ys[0, 1, pl.ds(w * WH, WH)] = made
            back[w] = push(
                ys.at[0, 1, pl.ds(w * WH, rows)], xs.at[1, 1, pl.ds(SH + w * WH, rows)], 0, -1)

        return done

    def send_corner():
        back["corner"] = push(
            ys.at[0, 1, pl.ds(body, SH)], xs.at[1, 1, pl.ds(0, SH)], 1, -1)

    def keep_own(w):
        rows = WH if w < count - 1 else WH - SH

        def done(made):
            xs[1, 0, pl.ds(SH + w * WH, rows)] = made[:rows]
            if w == count - 1:
                ys[0, 0, pl.ds(body, SH)] = made[rows:]
                back["lat"] = push(
                    ys.at[0, 0, pl.ds(body, SH)], xs.at[1, 0, pl.ds(0, SH)], 1, 0)

        return done

    def give(w, h):
        def done(made):
            out[pl.ds(w * WH, WH), pl.ds(SW * h, SW), :] = made

        return done

    waiting = None
    for w in range(count):
        for copy in got[w]:
            copy.wait_recv()
        project(0, w, 1)
        together(attend(0, w, 1, 0), *([waiting] if waiting else []))
        if w == 0:
            for name in ("out", "up", "down"):
                weights[name, 0].wait()
        together(attend(0, w, 0, 1), finish(0, w, 1, 0, send_west(w)))
        waiting = finish(0, w, 0, 1, keep_own(w))
    weights["in", 1].wait()
    for w in range(count):
        make_bias(1, w)
    together(waiting)

    for name in ("out", "up", "down"):
        weights[name, 1].wait()
    for w in reversed(range(count)):
        if w == 0:
            back["lat"].wait_recv()
        project(1, w, 0)
        if w == count - 1:
            send_corner()
    waiting = None
    waited = set()
    for w in reversed(range(count)):
        for v in (w - 1, w):
            if v >= 0 and v not in waited:
                waited.add(v)
                back[v].wait_recv()
        if w == 0:
            back["corner"].wait_recv()
        project(1, w, 1)
        together(attend(1, w, 0, 0), *([waiting] if waiting else []))
        together(attend(1, w, 1, 1), finish(1, w, 0, 0, give(w, 0)))
        waiting = finish(1, w, 1, 1, give(w, 1))
    together(waiting)
    for copy in sent:
        if copy is not got[0][0]:
            copy.wait_send()


def solution(mesh):
    names = tuple(mesh.axis_names)
    sizes = dict(mesh.shape)

    def on_device(atm, band, valid, gains, w_in, w_out, w_up, w_down):
        height, breadth, width = atm.shape
        hidden = w_up.shape[2]
        count = height // WH
        cells = WH * SW
        pairs = width // 128
        chunks = height // SH
        anyspace = pl.BlockSpec(memory_space=pl.ANY)
        vmem = pl.BlockSpec(memory_space=pltpu.VMEM)
        pushes = 2 * count + 7
        return pl.pallas_call(
            functools.partial(kernel, names, sizes),
            out_shape=pltpu.VMEM(atm.shape, BF16),
            in_specs=[anyspace] * 8,
            out_specs=vmem,
            scratch_shapes=[
                pltpu.VMEM((2, 2, height, SW, width), BF16),
                pltpu.VMEM((1, 2, height, SW, width), BF16),
                pltpu.VMEM((2, chunks, 8, SH * SW), jnp.int32),
                pltpu.VMEM((2, chunks, 8, SH * SW), jnp.int32),
                pltpu.VMEM((1, height), jnp.int32),
                pltpu.VMEM((breadth, height), jnp.int32),
                pltpu.VMEM(gains.shape, F32),
                pltpu.VMEM(w_in.shape, BF16),
                pltpu.VMEM(w_out.shape, BF16),
                pltpu.VMEM(w_up.shape, BF16),
                pltpu.VMEM(w_down.shape, BF16),
                pltpu.VMEM((count, pairs, 2, 2 * cells, 128), BF16),
                pltpu.VMEM((count, pairs, 2 * cells, 128), BF16),
                pltpu.VMEM((count, 2 * pairs, 80, 2 * cells), BF16),
                pltpu.VMEM((count, 2 * cells, 2 * cells), F32),
                pltpu.VMEM((2, width, cells), F32),
                pltpu.SemaphoreType.DMA((pushes,)),
                pltpu.SemaphoreType.DMA((pushes,)),
                pltpu.SemaphoreType.DMA((12,)),
            ],
            compiler_params=pltpu.CompilerParams(
                collective_id=0, has_side_effects=True, vmem_limit_bytes=56 * 1024 * 1024
            ),
        )(atm, band[None, :], valid.T, gains, w_in, w_out, w_up, w_down)

    rows = P(("groups", "lat"), "lon", None)
    return jax.shard_map(
        on_device,
        mesh=mesh,
        in_specs=(rows, P(("groups", "lat")), P(("groups", "lat"), "lon"), P(), P(), P(), P(), P()),
        out_specs=rows,
        check_vma=False,
    )
```

```python
import functools
import math

import jax
import jax.numpy as jnp
from jax import lax
from jax.experimental import pallas as pl
from jax.experimental.pallas import tpu as pltpu
from jax.sharding import PartitionSpec as P

H = 8
WH = 32
SH = 16
SW = 8
EPS = 1e-05
MESH = pl.DeviceIdType.MESH
F32 = jnp.float32
BF16 = jnp.bfloat16
BAND_BITS = 7
FAR = -1e30
DEPTH = 3


def norm(wide, gains):
    centred = wide - jnp.mean(wide, -1, keepdims=True)
    spread = jnp.mean(centred * centred, -1, keepdims=True)
    return (centred * lax.rsqrt(spread + EPS) * gains).astype(BF16)


def gelu_of_twice(u):
    root = math.sqrt(2.0 / math.pi)
    inner = u * (2.0 * root + (8.0 * root * 0.044715) * (u * u))
    return u + u * jnp.tanh(inner)


def kernel(
    names, sizes, atm, band_in, valid_in, gains_in, w_in, w_out, w_up, w_down, out,
    xs, ys, code, cs, band, valid, gains, win, wout, wup, wdown, q2, ks, vs, mask, acc, ctx,
    send, recv, local,
):
    height = atm.shape[0]
    width = atm.shape[2]
    count = height // WH
    cells = WH * SW
    pairs = width // 128
    body = height - SH
    last = height // SH - 1
    at = {name: lax.axis_index(name) for name in names}

    def device(lat, lon):
        spot = dict(at)
        spot["lat"] = lax.rem(at["lat"] + lat + sizes["lat"], sizes["lat"])
        spot["lon"] = lax.rem(at["lon"] + lon + sizes["lon"], sizes["lon"])
        return tuple(spot[name] for name in names)

    barrier = pltpu.get_barrier_semaphore()
    sources = ((1, 0), (0, -1), (1, -1))
    for lat, lon in sources:
        pl.semaphore_signal(barrier, inc=1, device_id=device(lat, lon), device_id_type=MESH)

    loads = []

    def load(src, dst):
        copy = pltpu.make_async_copy(src, dst, local.at[len(loads)])
        copy.start()
        loads.append(copy)
        return copy

    west, east = pl.ds(0, SW), pl.ds(SW, SW)
    small = [load(band_in, band), load(valid_in, valid), load(gains_in, gains)]
    own = load(atm.at[pl.ds(SH, body), west, :], xs.at[0, 0, pl.ds(0, body)])
    weights = {}
    for layer in range(2):
        for name, src, dst in (
            ("in", w_in, win), ("out", w_out, wout), ("up", w_up, wup), ("down", w_down, wdown),
        ):
            weights[name, layer] = load(src.at[layer], dst.at[layer])

    for copy in small:
        copy.wait()
    mixed = (2 * band[...] + valid[...]).astype(F32).astype(BF16)
    lane = lax.broadcasted_iota(jnp.int32, (mixed.shape[0], SH * SW), 1)
    column = lax.broadcasted_iota(jnp.int32, (mixed.shape[0], SH * SW), 0)
    lane_row = lax.broadcasted_iota(jnp.int32, (SH, SH * SW), 1) // SW
    keep = lane_row == lax.broadcasted_iota(jnp.int32, (SH, SH * SW), 0)
    for h in range(2):
        pick = jnp.where(column == lane % SW + SW * h, 1.0, 0.0).astype(BF16)
        spread = lax.dot_general(
            mixed, pick, (((0,), (0,)), ((), ())), preferred_element_type=F32)
        for chunk in range(last + 1):
            rows = jnp.where(keep, spread[SH * chunk:SH * chunk + SH], 0.0)
            rows = jnp.sum(rows, 0, keepdims=True).astype(jnp.int32)
            code[h, chunk] = jnp.broadcast_to(rows, (8, SH * SW))

    pl.semaphore_wait(barrier, len(sources))

    sent = []

    def push(src, dst, lat, lon):
        copy = pltpu.make_async_remote_copy(
            src_ref=src, dst_ref=dst, send_sem=send.at[len(sent)], recv_sem=recv.at[len(sent)],
            device_id=device(lat, lon), device_id_type=MESH,
        )
        copy.start()
        sent.append(copy)
        return copy

    got_code = [
        push(code.at[1, pl.ds(1, last)], cs.at[1, pl.ds(0, last)], 0, 1),
        push(code.at[0, pl.ds(0, 1)], cs.at[0, pl.ds(last, 1)], -1, 0),
        push(code.at[1, pl.ds(0, 1)], cs.at[1, pl.ds(last, 1)], -1, 1),
    ]
    got = []
    for w in range(count):
        rows = WH if w < count - 1 else WH - SH
        got.append([push(
            atm.at[pl.ds(SH + w * WH, rows), east, :], xs.at[0, 1, pl.ds(w * WH, rows)], 0, 1)])
    got_lat = push(atm.at[pl.ds(0, SH), west, :], xs.at[0, 0, pl.ds(body, SH)], -1, 0)

    vs[:, :, pl.ds(64, 16), :] = jnp.ones(vs.shape[:2] + (16, vs.shape[3]), BF16)
    low = lax.broadcasted_iota(jnp.int32, (cells, 128), 1) < 64
    scale = math.log2(math.e) / math.sqrt(64)

    def codes_of(layer, w, h):
        found = []
        for chunk in (2 * w, 2 * w + 1):
            if layer == 1:
                found.append(code[h, chunk])
            elif h == 0 and chunk < last:
                found.append(code[0, chunk + 1])
            else:
                found.append(cs[h, chunk])
        return found

    place_bits = (2 * cells - 1).bit_length()
    lanes_used = 2 * (BAND_BITS + place_bits)
    feature = lax.broadcasted_iota(jnp.int32, (128, 128), 1) & 63
    of_band = feature < 2 * BAND_BITS
    used = feature < lanes_used
    pol = feature & 1
    which = jnp.where(of_band, feature // 2 + 1, (feature - 2 * BAND_BITS) // 2)
    weight = jnp.zeros((128, 128), jnp.int32)
    for b in range(max(BAND_BITS + 1, place_bits)):
        weight = jnp.where(which == b, 1 << b, weight)
    weight = jnp.where(used, weight, 0)
    place = lax.broadcasted_iota(jnp.int32, (128, 128), 0)

    def make_mask(layer, w, h):
        for i, one in enumerate(codes_of(layer, w, h)):
            down = jnp.broadcast_to(one[0:1].astype(F32), (128, 128)).T.astype(jnp.int32)
            start = h * cells + 128 * i
            bit = jnp.where((jnp.where(of_band, down, place + start) & weight) != 0, 1, 0)
            match = bit == pol
            counts = used & (of_band | ((down & 1) == 0))
            mask[w, 0, pl.ds(start, 128), :] = jnp.where(match & counts, 1.0, 0.0)
            mask[w, 1, pl.ds(start, 128), :] = jnp.where(match | (feature >= lanes_used), 0.0, FAR)

    def field(layer, w, h, first=0, rows=WH):
        found = xs[layer, h, pl.ds(w * WH + first, rows)]
        return found.astype(F32).reshape(rows * SW, width)

    def project(layer, w, h, first=0, rows=WH):
        def steps():
            normed = norm(field(layer, w, h, first, rows), gains[layer, 0:1, :])
            size = rows * SW
            where = pl.ds(h * cells + first * SW, size)
            yield
            for part in range(3):
                made = jnp.dot(
                    normed, win[layer, :, pl.ds(part * width, width)], preferred_element_type=F32)
                if part == 2:
                    turned = made.T.astype(BF16)
                    for head in range(2 * pairs):
                        vs[w, head, pl.ds(0, 64), where] = turned[64 * head:64 * head + 64]
                    yield
                    continue
                extra = mask[w, 1 - part, where, :]
                for p in range(pairs):
                    two = made[:, 128 * p:128 * p + 128]
                    dst = ks
                    if part == 0:
                        two = two * scale
                        dst = q2
                    dst[w, 2 * p, where, :] = jnp.where(low[:size], two, extra).astype(BF16)
                    dst[w, 2 * p + 1, where, :] = jnp.where(low[:size], extra, two).astype(BF16)
                yield

        return 4, steps()

    heads = 2 * pairs

    def score(w, j, h, c):
        return lax.dot_general(
            ks[w, j, pl.ds(cells * c, cells), :], q2[w, j, pl.ds(cells * h, cells), :],
            (((1,), (1,)), ((), ())), preferred_element_type=F32)

    def weigh(w, j, c, made, top):
        raw = jnp.exp2(made - top).astype(BF16)
        return jnp.dot(
            vs[w, j, :, pl.ds(cells * c, cells)], raw, preferred_element_type=F32)

    def attend(w, h):
        flight = []

        def close():
            j, made, tops = flight.pop(0)
            top = jnp.maximum(tops[0], tops[1])
            total = weigh(w, j, 0, made[0], top) + weigh(w, j, 1, made[1], top)
            ctx[2 * w + h, pl.ds(64 * j, 64), :] = total[:64] / total[64:65]

        def steps():
            for j in range(heads):
                made = [score(w, j, h, c) for c in range(2)]
                flight.append((j, made, [jnp.max(one, 0, keepdims=True) for one in made]))
                if len(flight) > DEPTH:
                    close()
                yield
            while flight:
                close()
                yield

        return heads + DEPTH, steps()

    def attend_half(units, c, close):
        flight = []

        def end():
            w, j, made, top = flight.pop(0)
            close(w, j, weigh(w, j, c, made, top), top)

        def steps():
            for w, j in units:
                made = score(w, j, 0, c)
                flight.append((w, j, made, jnp.max(made, 0, keepdims=True)))
                if len(flight) > 2 * DEPTH:
                    end()
                yield
            while flight:
                end()
                yield

        return len(units) + 2 * DEPTH, steps()

    def attend_own(*windows):
        def close(w, j, part, top):
            acc[w, j, pl.ds(0, 72), :] = part[:72]
            acc[w, j, pl.ds(72, 8), :] = jnp.broadcast_to(top, (8, cells))

        return attend_half([(w, j) for w in windows for j in range(heads)], 0, close)

    def attend_rest(w):
        def close(w, j, part, top):
            first = acc[w, j, pl.ds(0, 64), :]
            first_sum = acc[w, j, pl.ds(64, 8), :][0:1]
            first_top = acc[w, j, pl.ds(72, 8), :][0:1]
            joint = jnp.maximum(first_top, top)
            mine, theirs = jnp.exp2(first_top - joint), jnp.exp2(top - joint)
            share = 1.0 / (first_sum * mine + part[64:65] * theirs)
            ctx[2 * w, pl.ds(64 * j, 64), :] = (
                first * (mine * share) + part[:64] * (theirs * share))

        return attend_half([(w, j) for j in range(heads)], 1, close)

    def finish(layer, w, h, done):
        step = 256

        def steps():
            turned = ctx[2 * w + h].T.astype(BF16)
            own_field = field(layer, w, h)
            parts = []
            for n in range(0, width, step):
                parts.append(own_field[:, n:n + step] + jnp.dot(
                    turned, wout[layer, :, pl.ds(n, step)], preferred_element_type=F32))
                yield
            resid = jnp.concatenate(parts, 1).astype(BF16).astype(F32)
            normed = norm(resid, 0.5 * gains[layer, 1:2, :])
            yield
            hidden = []
            for n in range(0, wup.shape[2], step):
                hidden.append(gelu_of_twice(jnp.dot(
                    normed, wup[layer, :, pl.ds(n, step)], preferred_element_type=F32)).astype(BF16))
                yield
            hidden = jnp.concatenate(hidden, 1)
            parts = []
            for n in range(0, width, step):
                parts.append(resid[:, n:n + step] + jnp.dot(
                    hidden, wdown[layer, :, pl.ds(n, step)], preferred_element_type=F32))
                yield
            done(jnp.concatenate(parts, 1).reshape(WH, SW, width).astype(BF16))

        return 1 + (2 * width + wup.shape[2]) // step, steps()

    def masks(layer):
        def steps():
            for w in range(count):
                for h in range(2):
                    make_mask(layer, w, h)
                    yield

        return 2 * count, steps()

    def chain(*works):
        def steps():
            for _, work in works:
                yield from work

        return sum(size for size, _ in works), steps()

    def together(*works):
        left = [[0, size, work] for size, work in works]
        while left:
            one = min(left, key=lambda it: (it[0] + 1) / it[1])
            one[0] += 1
            if next(one[2], left) is left:
                left.remove(one)

    own.wait()
    weights["in", 0].wait()
    for w in range(count - 1):
        make_mask(0, w, 0)
        together(project(0, w, 0))
    got_code[1].wait_recv()
    make_mask(0, count - 1, 0)
    got_lat.wait_recv()
    together(project(0, count - 1, 0))
    together(attend_own(*range(count)))
    got_code[0].wait_recv()
    got_code[2].wait_recv()
    for w in range(count):
        make_mask(0, w, 1)
    got[0][0].wait_send()
    got[count - 1].append(push(
        atm.at[pl.ds(0, SH), east, :], xs.at[0, 1, pl.ds(body, SH)], -1, 1))
    back = {}

    def send_west(w):
        rows = WH if w < count - 1 else WH - SH

        def done(made):
            ys[0, 1, pl.ds(w * WH, WH)] = made
            back[w] = push(
                ys.at[0, 1, pl.ds(w * WH, rows)], xs.at[1, 1, pl.ds(SH + w * WH, rows)], 0, -1)

        return done

    def send_corner():
        back["corner"] = push(
            ys.at[0, 1, pl.ds(body, SH)], xs.at[1, 1, pl.ds(0, SH)], 1, -1)

    def keep_own(w):
        rows = WH if w < count - 1 else WH - SH

        def done(made):
            xs[1, 0, pl.ds(SH + w * WH, rows)] = made[:rows]
            if w == count - 1:
                ys[0, 0, pl.ds(body, SH)] = made[rows:]
                back["lat"] = push(
                    ys.at[0, 0, pl.ds(body, SH)], xs.at[1, 0, pl.ds(0, SH)], 1, 0)

        return done

    def give(w, h):
        def done(made):
            out[pl.ds(w * WH, WH), pl.ds(SW * h, SW), :] = made

        return done

    waiting = []
    for w in range(count):
        for copy in got[w]:
            copy.wait_recv()
        together(project(0, w, 1), *waiting)
        together(attend(w, 1))
        if w == 0:
            for name in ("out", "up", "down"):
                weights[name, 0].wait()
        away, kept = finish(0, w, 1, send_west(w)), finish(0, w, 0, keep_own(w))
        together(attend_rest(w), away)
        waiting = [kept]
    weights["in", 1].wait()
    early = [project(1, w, 0, SH * (w == 0), SH) for w in (0, count - 1)]
    early = early + [project(1, w, 0) for w in range(1, count - 1)]
    together(kept, chain(masks(1), *early))
    for name in ("out", "up", "down"):
        weights[name, 1].wait()
    send_corner()
    together(project(1, count - 1, 0, SH, SH))
    together(attend_own(*range(1, count)))
    back["lat"].wait_recv()
    together(project(1, 0, 0, 0, SH))
    together(attend_own(0))
    waited = set()
    waiting = []
    for w in reversed(range(count)):
        for v in (w - 1, w):
            if v >= 0 and v not in waited:
                waited.add(v)
                back[v].wait_recv()
        if w == 0:
            back["corner"].wait_recv()
        together(project(1, w, 1), *waiting[:1])
        together(chain(attend(w, 1), attend_rest(w)), *waiting[1:])
        waiting = [finish(1, w, 1, give(w, 1)), finish(1, w, 0, give(w, 0))]
    together(*waiting)
    for copy in sent:
        if copy is not got[0][0]:
            copy.wait_send()


def solution(mesh):
    names = tuple(mesh.axis_names)
    sizes = dict(mesh.shape)

    def on_device(atm, band, valid, gains, w_in, w_out, w_up, w_down):
        height, breadth, width = atm.shape
        hidden = w_up.shape[2]
        count = height // WH
        cells = WH * SW
        pairs = width // 128
        chunks = height // SH
        anyspace = pl.BlockSpec(memory_space=pl.ANY)
        vmem = pl.BlockSpec(memory_space=pltpu.VMEM)
        pushes = 2 * count + 7
        return pl.pallas_call(
            functools.partial(kernel, names, sizes),
            out_shape=pltpu.VMEM(atm.shape, BF16),
            in_specs=[anyspace] * 8,
            out_specs=vmem,
            scratch_shapes=[
                pltpu.VMEM((2, 2, height, SW, width), BF16),
                pltpu.VMEM((1, 2, height, SW, width), BF16),
                pltpu.VMEM((2, chunks, 8, SH * SW), jnp.int32),
                pltpu.VMEM((2, chunks, 8, SH * SW), jnp.int32),
                pltpu.VMEM((1, height), jnp.int32),
                pltpu.VMEM((breadth, height), jnp.int32),
                pltpu.VMEM(gains.shape, F32),
                pltpu.VMEM(w_in.shape, BF16),
                pltpu.VMEM(w_out.shape, BF16),
                pltpu.VMEM(w_up.shape, BF16),
                pltpu.VMEM(w_down.shape, BF16),
                pltpu.VMEM((count, 2 * pairs, 2 * cells, 128), BF16),
                pltpu.VMEM((count, 2 * pairs, 2 * cells, 128), BF16),
                pltpu.VMEM((count, 2 * pairs, 80, 2 * cells), BF16),
                pltpu.VMEM((count, 2, 2 * cells, 128), F32),
                pltpu.VMEM((count, 2 * pairs, 80, cells), F32),
                pltpu.VMEM((2 * count, width, cells), F32),
                pltpu.SemaphoreType.DMA((pushes,)),
                pltpu.SemaphoreType.DMA((pushes,)),
                pltpu.SemaphoreType.DMA((12,)),
            ],
            compiler_params=pltpu.CompilerParams(
                collective_id=0, has_side_effects=True, vmem_limit_bytes=56 * 1024 * 1024
            ),
        )(atm, band[None, :], valid.T, gains, w_in, w_out, w_up, w_down)

    rows = P(("groups", "lat"), "lon", None)
    return jax.shard_map(
        on_device,
        mesh=mesh,
        in_specs=(rows, P(("groups", "lat")), P(("groups", "lat"), "lon"), P(), P(), P(), P(), P()),
        out_specs=rows,
        check_vma=False,
    )
```

```python
import functools
import math

import jax
import jax.numpy as jnp
from jax import lax
from jax.experimental import pallas as pl
from jax.experimental.pallas import tpu as pltpu
from jax.sharding import PartitionSpec as P

H = 8
WH = 32
SH = 16
SW = 8
EPS = 1e-05
MESH = pl.DeviceIdType.MESH
F32 = jnp.float32
BF16 = jnp.bfloat16
BAND_BITS = 7
FAR = -1e30
UNITS = 8


def norm(wide, gains):
    centred = wide - jnp.mean(wide, -1, keepdims=True)
    spread = jnp.mean(centred * centred, -1, keepdims=True)
    return (centred * lax.rsqrt(spread + EPS) * gains).astype(BF16)


def gelu_of_twice(u):
    root = math.sqrt(2.0 / math.pi)
    inner = u * (2.0 * root + (8.0 * root * 0.044715) * (u * u))
    return u + u * jnp.tanh(inner)


def kernel(
    names, sizes, atm, band_in, valid_in, gains_in, w_in, w_out, w_up, w_down, out,
    xs, ys, code, cs, band, valid, gains, win, wout, wup, wdown, q2, ks, vs, mask, acc, ctx,
    send, recv, local,
):
    height = atm.shape[0]
    width = atm.shape[2]
    count = height // WH
    cells = WH * SW
    pairs = width // 128
    body = height - SH
    last = height // SH - 1
    at = {name: lax.axis_index(name) for name in names}

    def device(lat, lon):
        spot = dict(at)
        spot["lat"] = lax.rem(at["lat"] + lat + sizes["lat"], sizes["lat"])
        spot["lon"] = lax.rem(at["lon"] + lon + sizes["lon"], sizes["lon"])
        return tuple(spot[name] for name in names)

    barrier = pltpu.get_barrier_semaphore()
    sources = ((1, 0), (0, -1), (1, -1))
    for lat, lon in sources:
        pl.semaphore_signal(barrier, inc=1, device_id=device(lat, lon), device_id_type=MESH)

    loads = []

    def load(src, dst):
        copy = pltpu.make_async_copy(src, dst, local.at[len(loads)])
        copy.start()
        loads.append(copy)
        return copy

    west, east = pl.ds(0, SW), pl.ds(SW, SW)
    small = [load(band_in, band), load(valid_in, valid), load(gains_in, gains)]
    own = load(atm.at[pl.ds(SH, body), west, :], xs.at[0, 0, pl.ds(0, body)])
    weights = {}
    for layer in range(2):
        for name, src, dst in (
            ("in", w_in, win), ("out", w_out, wout), ("up", w_up, wup), ("down", w_down, wdown),
        ):
            weights[name, layer] = load(src.at[layer], dst.at[layer])

    pl.semaphore_wait(barrier, len(sources))

    sent = []

    def push(src, dst, lat, lon):
        copy = pltpu.make_async_remote_copy(
            src_ref=src, dst_ref=dst, send_sem=send.at[len(sent)], recv_sem=recv.at[len(sent)],
            device_id=device(lat, lon), device_id_type=MESH,
        )
        copy.start()
        sent.append(copy)
        return copy

    def push_piece(w, first, rows):
        return push(
            atm.at[pl.ds(SH + w * WH + first, rows), east, :],
            xs.at[0, 1, pl.ds(w * WH + first, rows)], 0, 1)

    got = [[] for _ in range(count)]
    whole = [WH if w < count - 1 else WH - SH for w in range(count)]
    got[0].append(push_piece(0, 0, SH // 2))
    got_lat = push(atm.at[pl.ds(0, SH), west, :], xs.at[0, 0, pl.ds(body, SH)], -1, 0)

    for copy in small:
        copy.wait()
    mixed = (2 * band[...] + valid[...]).astype(F32).astype(BF16)
    lane = lax.broadcasted_iota(jnp.int32, (mixed.shape[0], SH * SW), 1)
    column = lax.broadcasted_iota(jnp.int32, (mixed.shape[0], SH * SW), 0)
    lane_row = lax.broadcasted_iota(jnp.int32, (SH, SH * SW), 1) // SW
    keep = lane_row == lax.broadcasted_iota(jnp.int32, (SH, SH * SW), 0)
    for h in range(2):
        pick = jnp.where(column == lane % SW + SW * h, 1.0, 0.0).astype(BF16)
        spread = lax.dot_general(
            mixed, pick, (((0,), (0,)), ((), ())), preferred_element_type=F32)
        for chunk in range(last + 1):
            rows = jnp.where(keep, spread[SH * chunk:SH * chunk + SH], 0.0)
            rows = jnp.sum(rows, 0, keepdims=True).astype(jnp.int32)
            code[h, chunk] = jnp.broadcast_to(rows, (8, SH * SW))

    got_code = [
        push(code.at[1, pl.ds(1, last)], cs.at[1, pl.ds(0, last)], 0, 1),
        push(code.at[0, pl.ds(0, 1)], cs.at[0, pl.ds(last, 1)], -1, 0),
        push(code.at[1, pl.ds(0, 1)], cs.at[1, pl.ds(last, 1)], -1, 1),
    ]
    got[0].append(push_piece(0, SH // 2, SH // 2))
    if whole[0] > SH:
        got[0].append(push_piece(0, SH, SH))
    for w in range(1, count):
        got[w].append(push_piece(w, 0, whole[w]))

    vs[:, :, pl.ds(64, 16), :] = jnp.ones(vs.shape[:2] + (16, vs.shape[3]), BF16)
    low = lax.broadcasted_iota(jnp.int32, (cells, 128), 1) < 64
    scale = math.log2(math.e) / math.sqrt(64)

    def codes_of(layer, w, h):
        found = []
        for chunk in (2 * w, 2 * w + 1):
            if layer == 1:
                found.append(code[h, chunk])
            elif h == 0 and chunk < last:
                found.append(code[0, chunk + 1])
            else:
                found.append(cs[h, chunk])
        return found

    place_bits = (2 * cells - 1).bit_length()
    lanes_used = 2 * (BAND_BITS + place_bits)
    feature = lax.broadcasted_iota(jnp.int32, (128, 128), 1) & 63
    of_band = feature < 2 * BAND_BITS
    used = feature < lanes_used
    pol = feature & 1
    which = jnp.where(of_band, feature // 2 + 1, (feature - 2 * BAND_BITS) // 2)
    weight = jnp.zeros((128, 128), jnp.int32)
    for b in range(max(BAND_BITS + 1, place_bits)):
        weight = jnp.where(which == b, 1 << b, weight)
    weight = jnp.where(used, weight, 0)
    place = lax.broadcasted_iota(jnp.int32, (128, 128), 0)

    def make_mask(layer, w, h):
        for i, one in enumerate(codes_of(layer, w, h)):
            down = jnp.broadcast_to(one[0:1].astype(F32), (128, 128)).T.astype(jnp.int32)
            start = h * cells + 128 * i
            bit = jnp.where((jnp.where(of_band, down, place + start) & weight) != 0, 1, 0)
            match = bit == pol
            counts = used & (of_band | ((down & 1) == 0))
            mask[w, 0, pl.ds(start, 128), :] = jnp.where(match & counts, 1.0, 0.0)
            mask[w, 1, pl.ds(start, 128), :] = jnp.where(match | (feature >= lanes_used), 0.0, FAR)

    def field(layer, w, h, first=0, rows=WH):
        found = xs[layer, h, pl.ds(w * WH + first, rows)]
        return found.astype(F32).reshape(rows * SW, width)

    def project(layer, w, h, first=0, rows=WH):
        def steps():
            normed = norm(field(layer, w, h, first, rows), gains[layer, 0:1, :])
            size = rows * SW
            where = pl.ds(h * cells + first * SW, size)
            yield
            for part in range(3):
                made = jnp.dot(
                    normed, win[layer, :, pl.ds(part * width, width)], preferred_element_type=F32)
                if part == 2:
                    turned = made.T.astype(BF16)
                    for head in range(2 * pairs):
                        vs[w, head, pl.ds(0, 64), where] = turned[64 * head:64 * head + 64]
                    yield
                    continue
                extra = mask[w, 1 - part, where, :]
                for p in range(pairs):
                    two = made[:, 128 * p:128 * p + 128]
                    dst = ks
                    if part == 0:
                        two = two * scale
                        dst = q2
                    dst[w, 2 * p, where, :] = jnp.where(low[:size], two, extra).astype(BF16)
                    dst[w, 2 * p + 1, where, :] = jnp.where(low[:size], extra, two).astype(BF16)
                yield

        return 4, steps()

    heads = 2 * pairs

    def score(w, j, h, c):
        return lax.dot_general(
            ks[w, j, pl.ds(cells * c, cells), :], q2[w, j, pl.ds(cells * h, cells), :],
            (((1,), (1,)), ((), ())), preferred_element_type=F32)

    def weigh(w, j, c, made, top):
        raw = jnp.exp2(made - top).astype(BF16)
        return jnp.dot(
            vs[w, j, :, pl.ds(cells * c, cells)], raw, preferred_element_type=F32)

    def pipeline(items):
        def steps():
            flight = []
            for size, begin, end in items:
                flight.append((size, end, begin()))
                while sum(one[0] for one in flight) > UNITS:
                    _, close, state = flight.pop(0)
                    close(*state)
                yield
            for _, close, state in flight:
                close(*state)
                yield

        return len(items) + UNITS // items[-1][0], steps()

    def whole_item(w, j):
        def begin():
            made = [score(w, j, 1, c) for c in range(2)]
            return made, [jnp.max(one, 0, keepdims=True) for one in made]

        def end(made, tops):
            top = jnp.maximum(tops[0], tops[1])
            total = weigh(w, j, 0, made[0], top) + weigh(w, j, 1, made[1], top)
            ctx[2 * w + 1, pl.ds(64 * j, 64), :] = total[:64] / total[64:65]

        return 2, begin, end

    def half_item(w, j, c, close):
        def begin():
            made = score(w, j, 0, c)
            return made, jnp.max(made, 0, keepdims=True)

        def end(made, top):
            close(weigh(w, j, c, made, top), top)

        return 1, begin, end

    def own_item(w, j):
        def close(part, top):
            acc[w, j, pl.ds(0, 72), :] = part[:72]
            acc[w, j, pl.ds(72, 8), :] = jnp.broadcast_to(top, (8, cells))

        return half_item(w, j, 0, close)

    def rest_item(w, j):
        def close(part, top):
            first = acc[w, j, pl.ds(0, 64), :]
            first_sum = acc[w, j, pl.ds(64, 8), :][0:1]
            first_top = acc[w, j, pl.ds(72, 8), :][0:1]
            joint = jnp.maximum(first_top, top)
            mine, theirs = jnp.exp2(first_top - joint), jnp.exp2(top - joint)
            share = 1.0 / (first_sum * mine + part[64:65] * theirs)
            ctx[2 * w, pl.ds(64 * j, 64), :] = (
                first * (mine * share) + part[:64] * (theirs * share))

        return half_item(w, j, 1, close)

    def attend(w):
        return pipeline([whole_item(w, j) for j in range(heads)])

    def attend_own(*windows):
        return pipeline([own_item(w, j) for w in windows for j in range(heads)])

    def attend_rest(w):
        return pipeline([rest_item(w, j) for j in range(heads)])

    def attend_both(w):
        return pipeline(
            [whole_item(w, j) for j in range(heads)] + [rest_item(w, j) for j in range(heads)])

    def finish(layer, w, h, done):
        step = 256

        def steps():
            turned = ctx[2 * w + h].T.astype(BF16)
            own_field = field(layer, w, h)
            parts = []
            for n in range(0, width, step):
                parts.append(own_field[:, n:n + step] + jnp.dot(
                    turned, wout[layer, :, pl.ds(n, step)], preferred_element_type=F32))
                yield
            resid = jnp.concatenate(parts, 1).astype(BF16).astype(F32)
            normed = norm(resid, 0.5 * gains[layer, 1:2, :])
            yield
            hidden = []
            for n in range(0, wup.shape[2], step):
                hidden.append(gelu_of_twice(jnp.dot(
                    normed, wup[layer, :, pl.ds(n, step)], preferred_element_type=F32)).astype(BF16))
                yield
            hidden = jnp.concatenate(hidden, 1)
            parts = []
            for n in range(0, width, step):
                parts.append(resid[:, n:n + step] + jnp.dot(
                    hidden, wdown[layer, :, pl.ds(n, step)], preferred_element_type=F32))
                yield
            done(jnp.concatenate(parts, 1).reshape(WH, SW, width).astype(BF16))

        return 1 + (2 * width + wup.shape[2]) // step, steps()

    def masks(layer):
        def steps():
            for w in range(count):
                for h in range(2):
                    make_mask(layer, w, h)
                    yield

        return 2 * count, steps()

    def chain(*works):
        def steps():
            for _, work in works:
                yield from work

        return max(1, sum(size for size, _ in works)), steps()

    def together(*works):
        left = [[0, size, work] for size, work in works]
        while left:
            one = min(left, key=lambda it: (it[0] + 1) / it[1])
            one[0] += 1
            if next(one[2], left) is left:
                left.remove(one)

    own.wait()
    weights["in", 0].wait()
    for w in range(count - 1):
        make_mask(0, w, 0)
        together(project(0, w, 0))
    got_code[1].wait_recv()
    make_mask(0, count - 1, 0)
    got_lat.wait_recv()
    together(project(0, count - 1, 0))
    together(attend_own(*range(count)))
    for name in ("out", "up", "down"):
        weights[name, 0].wait()
    got_code[0].wait_recv()
    got_code[2].wait_recv()
    for w in range(count):
        make_mask(0, w, 1)
    gone = list(got[0])
    for copy in gone:
        copy.wait_send()
    got[count - 1].append(push(
        atm.at[pl.ds(0, SH), east, :], xs.at[0, 1, pl.ds(body, SH)], -1, 1))
    back = {}

    def send_west(w):
        rows = WH if w < count - 1 else WH - SH

        def done(made):
            ys[0, 1, pl.ds(w * WH, WH)] = made
            back[w] = push(
                ys.at[0, 1, pl.ds(w * WH, rows)], xs.at[1, 1, pl.ds(SH + w * WH, rows)], 0, -1)

        return done

    def send_corner():
        back["corner"] = push(
            ys.at[0, 1, pl.ds(body, SH)], xs.at[1, 1, pl.ds(0, SH)], 1, -1)

    def keep_own(w):
        rows = WH if w < count - 1 else WH - SH

        def done(made):
            xs[1, 0, pl.ds(SH + w * WH, rows)] = made[:rows]
            if w == count - 1:
                ys[0, 0, pl.ds(body, SH)] = made[rows:]
                back["lat"] = push(
                    ys.at[0, 0, pl.ds(body, SH)], xs.at[1, 0, pl.ds(0, SH)], 1, 0)

        return done

    def give(w, h):
        def done(made):
            out[pl.ds(w * WH, WH), pl.ds(SW * h, SW), :] = made

        return done

    waiting = []
    for w in range(count):
        for copy in got[w][:-1]:
            copy.wait_recv()
        if len(got[w]) > 1:
            together(project(0, w, 1, 0, SH), *waiting)
            got[w][-1].wait_recv()
            together(project(0, w, 1, SH, SH))
        else:
            got[w][0].wait_recv()
            together(project(0, w, 1), *waiting)
        if w == count - 1:
            for name in ("in", "out", "up", "down"):
                weights[name, 1].wait()
        together(attend(w))
        away, kept = finish(0, w, 1, send_west(w)), finish(0, w, 0, keep_own(w))
        together(attend_rest(w), away)
        waiting = [kept]
    early = [project(1, w, 0, SH * (w == 0), SH) for w in (0, count - 1)]
    early = early + [project(1, w, 0) for w in range(1, count - 1)]
    together(kept, chain(masks(1), *early))
    together(project(1, count - 1, 0, SH, SH))
    together(attend_own(*range(1, count)))
    send_corner()
    back["lat"].wait_recv()
    for w in range(count - 1):
        back[w].wait_recv()
    together(
        chain(project(1, 0, 0, 0, SH), attend_own(0)),
        chain(*(project(1, w, 1, 0, SH) for w in reversed(range(1, count)))))
    back[count - 1].wait_recv()
    together(project(1, count - 1, 1, SH, SH))
    waiting = []
    for w in reversed(range(count)):
        if w == 0:
            back["corner"].wait_recv()
            together(project(1, w, 1, 0, SH), *waiting[:1])
            waiting = waiting[1:]
        ahead = [project(1, w - 1, 1, SH, SH)] if w > 0 else []
        together(attend_both(w), *ahead, *waiting)
        waiting = [finish(1, w, 1, give(w, 1)), finish(1, w, 0, give(w, 0))]
    together(*waiting)
    for copy in sent:
        if all(copy is not one for one in gone):
            copy.wait_send()


def solution(mesh):
    names = tuple(mesh.axis_names)
    sizes = dict(mesh.shape)

    def on_device(atm, band, valid, gains, w_in, w_out, w_up, w_down):
        height, breadth, width = atm.shape
        hidden = w_up.shape[2]
        count = height // WH
        cells = WH * SW
        pairs = width // 128
        chunks = height // SH
        anyspace = pl.BlockSpec(memory_space=pl.ANY)
        vmem = pl.BlockSpec(memory_space=pltpu.VMEM)
        pushes = 2 * count + 9
        return pl.pallas_call(
            functools.partial(kernel, names, sizes),
            out_shape=pltpu.VMEM(atm.shape, BF16),
            in_specs=[anyspace] * 8,
            out_specs=vmem,
            scratch_shapes=[
                pltpu.VMEM((2, 2, height, SW, width), BF16),
                pltpu.VMEM((1, 2, height, SW, width), BF16),
                pltpu.VMEM((2, chunks, 8, SH * SW), jnp.int32),
                pltpu.VMEM((2, chunks, 8, SH * SW), jnp.int32),
                pltpu.VMEM((1, height), jnp.int32),
                pltpu.VMEM((breadth, height), jnp.int32),
                pltpu.VMEM(gains.shape, F32),
                pltpu.VMEM(w_in.shape, BF16),
                pltpu.VMEM(w_out.shape, BF16),
                pltpu.VMEM(w_up.shape, BF16),
                pltpu.VMEM(w_down.shape, BF16),
                pltpu.VMEM((count, 2 * pairs, 2 * cells, 128), BF16),
                pltpu.VMEM((count, 2 * pairs, 2 * cells, 128), BF16),
                pltpu.VMEM((count, 2 * pairs, 80, 2 * cells), BF16),
                pltpu.VMEM((count, 2, 2 * cells, 128), F32),
                pltpu.VMEM((count, 2 * pairs, 80, cells), F32),
                pltpu.VMEM((2 * count, width, cells), F32),
                pltpu.SemaphoreType.DMA((pushes,)),
                pltpu.SemaphoreType.DMA((pushes,)),
                pltpu.SemaphoreType.DMA((12,)),
            ],
            compiler_params=pltpu.CompilerParams(
                collective_id=0, has_side_effects=True, vmem_limit_bytes=56 * 1024 * 1024
            ),
        )(atm, band[None, :], valid.T, gains, w_in, w_out, w_up, w_down)

    rows = P(("groups", "lat"), "lon", None)
    return jax.shard_map(
        on_device,
        mesh=mesh,
        in_specs=(rows, P(("groups", "lat")), P(("groups", "lat"), "lon"), P(), P(), P(), P(), P()),
        out_specs=rows,
        check_vma=False,
    )
```

```python
import functools
import math

import jax
import jax.numpy as jnp
from jax import lax
from jax.experimental import pallas as pl
from jax.experimental.pallas import tpu as pltpu
from jax.sharding import PartitionSpec as P

H = 8
WH = 32
SH = 16
SW = 8
EPS = 1e-05
MESH = pl.DeviceIdType.MESH
F32 = jnp.float32
BF16 = jnp.bfloat16
BAND_BITS = 7
FAR = -1e30
UNITS = 6


def norm(wide, gains):
    centred = wide - jnp.mean(wide, -1, keepdims=True)
    spread = jnp.mean(centred * centred, -1, keepdims=True)
    return (centred * lax.rsqrt(spread + EPS) * gains).astype(BF16)


def gelu_of_twice(u):
    root = math.sqrt(2.0 / math.pi)
    inner = u * (2.0 * root + (8.0 * root * 0.044715) * (u * u))
    return u + u * jnp.tanh(inner)


def kernel(
    names, sizes, atm, band_in, valid_in, gains_in, w_in, w_out, w_up, w_down, out,
    xs, ys, code, cs, band, valid, gains, win, wout, wup, wdown, q2, ks, vs, mask, acc, ctx,
    send, recv, local,
):
    height = atm.shape[0]
    width = atm.shape[2]
    count = height // WH
    cells = WH * SW
    pairs = width // 128
    body = height - SH
    last = height // SH - 1
    at = {name: lax.axis_index(name) for name in names}

    def device(lat, lon):
        spot = dict(at)
        spot["lat"] = lax.rem(at["lat"] + lat + sizes["lat"], sizes["lat"])
        spot["lon"] = lax.rem(at["lon"] + lon + sizes["lon"], sizes["lon"])
        return tuple(spot[name] for name in names)

    barrier = pltpu.get_barrier_semaphore()
    sources = ((1, 0), (0, -1), (1, -1))
    for lat, lon in sources:
        pl.semaphore_signal(barrier, inc=1, device_id=device(lat, lon), device_id_type=MESH)

    loads = []

    def load(src, dst):
        copy = pltpu.make_async_copy(src, dst, local.at[len(loads)])
        copy.start()
        loads.append(copy)
        return copy

    west, east = pl.ds(0, SW), pl.ds(SW, SW)
    small = [load(band_in, band), load(valid_in, valid), load(gains_in, gains)]
    own = load(atm.at[pl.ds(SH, body), west, :], xs.at[0, 0, pl.ds(0, body)])
    weights = {}
    for layer in range(2):
        for name, src, dst in (
            ("in", w_in, win), ("out", w_out, wout), ("up", w_up, wup), ("down", w_down, wdown),
        ):
            weights[name, layer] = load(src.at[layer], dst.at[layer])

    pl.semaphore_wait(barrier, len(sources))

    sent = []

    def push(src, dst, lat, lon):
        copy = pltpu.make_async_remote_copy(
            src_ref=src, dst_ref=dst, send_sem=send.at[len(sent)], recv_sem=recv.at[len(sent)],
            device_id=device(lat, lon), device_id_type=MESH,
        )
        copy.start()
        sent.append(copy)
        return copy

    def push_piece(w, first, rows):
        return push(
            atm.at[pl.ds(SH + w * WH + first, rows), east, :],
            xs.at[0, 1, pl.ds(w * WH + first, rows)], 0, 1)

    got = [[] for _ in range(count)]
    whole = [WH if w < count - 1 else WH - SH for w in range(count)]
    got[0].append(push_piece(0, 0, SH // 2))
    got_lat = push(atm.at[pl.ds(0, SH), west, :], xs.at[0, 0, pl.ds(body, SH)], -1, 0)

    for copy in small:
        copy.wait()
    mixed = (2 * band[...] + valid[...]).astype(F32).astype(BF16)
    lane = lax.broadcasted_iota(jnp.int32, (mixed.shape[0], SH * SW), 1)
    column = lax.broadcasted_iota(jnp.int32, (mixed.shape[0], SH * SW), 0)
    lane_row = lax.broadcasted_iota(jnp.int32, (SH, SH * SW), 1) // SW
    keep = lane_row == lax.broadcasted_iota(jnp.int32, (SH, SH * SW), 0)
    for h in range(2):
        pick = jnp.where(column == lane % SW + SW * h, 1.0, 0.0).astype(BF16)
        spread = lax.dot_general(
            mixed, pick, (((0,), (0,)), ((), ())), preferred_element_type=F32)
        for chunk in range(last + 1):
            rows = jnp.where(keep, spread[SH * chunk:SH * chunk + SH], 0.0)
            rows = jnp.sum(rows, 0, keepdims=True).astype(jnp.int32)
            code[h, chunk] = jnp.broadcast_to(rows, (8, SH * SW))

    got_code = [
        push(code.at[1, pl.ds(1, last)], cs.at[1, pl.ds(0, last)], 0, 1),
        push(code.at[0, pl.ds(0, 1)], cs.at[0, pl.ds(last, 1)], -1, 0),
        push(code.at[1, pl.ds(0, 1)], cs.at[1, pl.ds(last, 1)], -1, 1),
    ]
    got[0].append(push_piece(0, SH // 2, SH // 2))
    if whole[0] > SH:
        got[0].append(push_piece(0, SH, SH))
    for w in range(1, count):
        got[w].append(push_piece(w, 0, whole[w]))

    vs[:, :, pl.ds(64, 16), :] = jnp.ones(vs.shape[:2] + (16, vs.shape[3]), BF16)
    low = lax.broadcasted_iota(jnp.int32, (cells, 128), 1) < 64
    scale = math.log2(math.e) / math.sqrt(64)

    def codes_of(layer, w, h):
        found = []
        for chunk in (2 * w, 2 * w + 1):
            if layer == 1:
                found.append(code[h, chunk])
            elif h == 0 and chunk < last:
                found.append(code[0, chunk + 1])
            else:
                found.append(cs[h, chunk])
        return found

    place_bits = (2 * cells - 1).bit_length()
    lanes_used = 2 * (BAND_BITS + place_bits)
    feature = lax.broadcasted_iota(jnp.int32, (128, 128), 1) & 63
    of_band = feature < 2 * BAND_BITS
    used = feature < lanes_used
    pol = feature & 1
    which = jnp.where(of_band, feature // 2 + 1, (feature - 2 * BAND_BITS) // 2)
    weight = jnp.zeros((128, 128), jnp.int32)
    for b in range(max(BAND_BITS + 1, place_bits)):
        weight = jnp.where(which == b, 1 << b, weight)
    weight = jnp.where(used, weight, 0)
    place = lax.broadcasted_iota(jnp.int32, (128, 128), 0)

    def make_mask(layer, w, h):
        for i, one in enumerate(codes_of(layer, w, h)):
            down = jnp.broadcast_to(one[0:1].astype(F32), (128, 128)).T.astype(jnp.int32)
            start = h * cells + 128 * i
            bit = jnp.where((jnp.where(of_band, down, place + start) & weight) != 0, 1, 0)
            match = bit == pol
            counts = used & (of_band | ((down & 1) == 0))
            mask[w, 0, pl.ds(start, 128), :] = jnp.where(match & counts, 1.0, 0.0)
            mask[w, 1, pl.ds(start, 128), :] = jnp.where(match | (feature >= lanes_used), 0.0, FAR)

    def field(layer, w, h, first=0, rows=WH):
        found = xs[layer, h, pl.ds(w * WH + first, rows)]
        return found.astype(F32).reshape(rows * SW, width)

    def project(layer, w, h, first=0, rows=WH):
        def steps():
            normed = norm(field(layer, w, h, first, rows), gains[layer, 0:1, :])
            size = rows * SW
            where = pl.ds(h * cells + first * SW, size)
            yield
            for part in range(3):
                made = jnp.dot(
                    normed, win[layer, :, pl.ds(part * width, width)], preferred_element_type=F32)
                if part == 2:
                    turned = made.astype(BF16).T
                    for head in range(2 * pairs):
                        vs[w, head, pl.ds(0, 64), where] = turned[64 * head:64 * head + 64]
                    yield
                    continue
                extra = mask[w, 1 - part, where, :]
                for p in range(pairs):
                    two = made[:, 128 * p:128 * p + 128]
                    dst = ks
                    if part == 0:
                        two = two * scale
                        dst = q2
                    dst[w, 2 * p, where, :] = jnp.where(low[:size], two, extra).astype(BF16)
                    dst[w, 2 * p + 1, where, :] = jnp.where(low[:size], extra, two).astype(BF16)
                yield

        return 4, steps()

    heads = 2 * pairs

    def score(w, j, h, c):
        return lax.dot_general(
            ks[w, j, pl.ds(cells * c, cells), :], q2[w, j, pl.ds(cells * h, cells), :],
            (((1,), (1,)), ((), ())), preferred_element_type=F32)

    def weigh(w, j, c, made, top):
        raw = jnp.exp2(made - top).astype(BF16)
        return jnp.dot(
            vs[w, j, :, pl.ds(cells * c, cells)], raw, preferred_element_type=F32)

    def pipeline(items):
        def steps():
            flight = []
            for size, begin, end in items:
                flight.append((size, end, begin()))
                while sum(one[0] for one in flight) > UNITS:
                    _, close, state = flight.pop(0)
                    close(*state)
                yield
            for _, close, state in flight:
                close(*state)
                yield

        return len(items) + UNITS // items[-1][0], steps()

    def whole_item(w, j):
        def begin():
            made = [score(w, j, 1, c) for c in range(2)]
            return made, [jnp.max(one, 0, keepdims=True) for one in made]

        def end(made, tops):
            top = jnp.maximum(tops[0], tops[1])
            total = weigh(w, j, 0, made[0], top) + weigh(w, j, 1, made[1], top)
            ctx[2 * w + 1, pl.ds(64 * j, 64), :] = (total[:64] / total[64:65]).astype(BF16)

        return 2, begin, end

    def half_item(w, j, c, close):
        def begin():
            made = score(w, j, 0, c)
            return made, jnp.max(made, 0, keepdims=True)

        def end(made, top):
            close(weigh(w, j, c, made, top), top)

        return 1, begin, end

    def own_item(w, j):
        def close(part, top):
            acc[w, j, pl.ds(0, 72), :] = part[:72]
            acc[w, j, pl.ds(72, 8), :] = jnp.broadcast_to(top, (8, cells))

        return half_item(w, j, 0, close)

    def rest_item(w, j):
        def close(part, top):
            first = acc[w, j, pl.ds(0, 64), :]
            first_sum = acc[w, j, pl.ds(64, 8), :][0:1]
            first_top = acc[w, j, pl.ds(72, 8), :][0:1]
            joint = jnp.maximum(first_top, top)
            mine, theirs = jnp.exp2(first_top - joint), jnp.exp2(top - joint)
            share = 1.0 / (first_sum * mine + part[64:65] * theirs)
            ctx[2 * w, pl.ds(64 * j, 64), :] = (
                first * (mine * share) + part[:64] * (theirs * share)).astype(BF16)

        return half_item(w, j, 1, close)

    def attend(w):
        return pipeline([whole_item(w, j) for j in range(heads)])

    def attend_own(*windows):
        return pipeline([own_item(w, j) for w in windows for j in range(heads)])

    def attend_rest(w):
        return pipeline([rest_item(w, j) for j in range(heads)])

    def attend_both(w):
        return pipeline(
            [whole_item(w, j) for j in range(heads)] + [rest_item(w, j) for j in range(heads)])

    def finish(layer, w, h, done):
        step = 256

        def steps():
            turned = ctx[2 * w + h].T
            own_field = field(layer, w, h)
            parts = []
            for n in range(0, width, step):
                parts.append(own_field[:, n:n + step] + jnp.dot(
                    turned, wout[layer, :, pl.ds(n, step)], preferred_element_type=F32))
                yield
            resid = jnp.concatenate(parts, 1).astype(BF16).astype(F32)
            normed = norm(resid, 0.5 * gains[layer, 1:2, :])
            yield
            hidden = []
            for n in range(0, wup.shape[2], step):
                hidden.append(gelu_of_twice(jnp.dot(
                    normed, wup[layer, :, pl.ds(n, step)], preferred_element_type=F32)).astype(BF16))
                yield
            hidden = jnp.concatenate(hidden, 1)
            parts = []
            for n in range(0, width, step):
                parts.append(resid[:, n:n + step] + jnp.dot(
                    hidden, wdown[layer, :, pl.ds(n, step)], preferred_element_type=F32))
                yield
            done(jnp.concatenate(parts, 1).reshape(WH, SW, width).astype(BF16))

        return 1 + (2 * width + wup.shape[2]) // step, steps()

    def masks(layer):
        def steps():
            for w in range(count):
                for h in range(2):
                    make_mask(layer, w, h)
                    yield

        return 2 * count, steps()

    def chain(*works):
        def steps():
            for _, work in works:
                yield from work

        return max(1, sum(size for size, _ in works)), steps()

    def together(*works):
        left = [[0, size, work] for size, work in works]
        while left:
            one = min(left, key=lambda it: (it[0] + 1) / it[1])
            one[0] += 1
            if next(one[2], left) is left:
                left.remove(one)

    own.wait()
    weights["in", 0].wait()
    for w in range(count - 1):
        make_mask(0, w, 0)
        together(project(0, w, 0))
    got_code[1].wait_recv()
    make_mask(0, count - 1, 0)
    got_lat.wait_recv()
    together(project(0, count - 1, 0))
    together(attend_own(*range(count)))
    for name in ("out", "up", "down"):
        weights[name, 0].wait()
    got_code[0].wait_recv()
    got_code[2].wait_recv()
    for w in range(count):
        make_mask(0, w, 1)
    gone = list(got[0])
    for copy in gone:
        copy.wait_send()
    got[count - 1].append(push(
        atm.at[pl.ds(0, SH), east, :], xs.at[0, 1, pl.ds(body, SH)], -1, 1))
    back = {}

    def send_west(w):
        rows = WH if w < count - 1 else WH - SH

        def done(made):
            ys[0, 1, pl.ds(w * WH, WH)] = made
            back[w] = push(
                ys.at[0, 1, pl.ds(w * WH, rows)], xs.at[1, 1, pl.ds(SH + w * WH, rows)], 0, -1)

        return done

    def send_corner():
        back["corner"] = push(
            ys.at[0, 1, pl.ds(body, SH)], xs.at[1, 1, pl.ds(0, SH)], 1, -1)

    def keep_own(w):
        rows = WH if w < count - 1 else WH - SH

        def done(made):
            xs[1, 0, pl.ds(SH + w * WH, rows)] = made[:rows]
            if w == count - 1:
                ys[0, 0, pl.ds(body, SH)] = made[rows:]
                back["lat"] = push(
                    ys.at[0, 0, pl.ds(body, SH)], xs.at[1, 0, pl.ds(0, SH)], 1, 0)

        return done

    def give(w, h):
        def done(made):
            out[pl.ds(w * WH, WH), pl.ds(SW * h, SW), :] = made

        return done

    waiting = []
    for w in range(count):
        for copy in got[w][:-1]:
            copy.wait_recv()
        if len(got[w]) > 1:
            together(project(0, w, 1, 0, SH), *waiting)
            got[w][-1].wait_recv()
            together(project(0, w, 1, SH, SH))
        else:
            got[w][0].wait_recv()
            together(project(0, w, 1), *waiting)
        if w == count - 1:
            for name in ("in", "out", "up", "down"):
                weights[name, 1].wait()
        together(attend(w))
        away, kept = finish(0, w, 1, send_west(w)), finish(0, w, 0, keep_own(w))
        together(attend_rest(w), away)
        waiting = [kept]
    early = [project(1, w, 0, SH * (w == 0), SH) for w in (0, count - 1)]
    early = early + [project(1, w, 0) for w in range(1, count - 1)]
    together(kept, chain(masks(1), *early))
    together(project(1, count - 1, 0, SH, SH))
    together(attend_own(*range(1, count)))
    send_corner()
    back["lat"].wait_recv()
    for w in range(count - 1):
        back[w].wait_recv()
    together(
        chain(project(1, 0, 0, 0, SH), attend_own(0)),
        chain(*(project(1, w, 1, 0, SH) for w in reversed(range(1, count)))))
    back[count - 1].wait_recv()
    together(project(1, count - 1, 1, SH, SH))
    waiting = []
    for w in reversed(range(count)):
        if w == 0:
            back["corner"].wait_recv()
        first = [project(1, w, 1, 0, SH)] if w == 0 else []
        ahead = [project(1, w - 1, 1, SH, SH)] if w > 0 else []
        together(chain(*first, attend_both(w)), *ahead, *waiting)
        waiting = [finish(1, w, 1, give(w, 1)), finish(1, w, 0, give(w, 0))]
    together(*waiting)
    for copy in sent:
        if all(copy is not one for one in gone):
            copy.wait_send()


def solution(mesh):
    names = tuple(mesh.axis_names)
    sizes = dict(mesh.shape)

    def on_device(atm, band, valid, gains, w_in, w_out, w_up, w_down):
        height, breadth, width = atm.shape
        hidden = w_up.shape[2]
        count = height // WH
        cells = WH * SW
        pairs = width // 128
        chunks = height // SH
        anyspace = pl.BlockSpec(memory_space=pl.ANY)
        vmem = pl.BlockSpec(memory_space=pltpu.VMEM)
        pushes = 2 * count + 9
        return pl.pallas_call(
            functools.partial(kernel, names, sizes),
            out_shape=pltpu.VMEM(atm.shape, BF16),
            in_specs=[anyspace] * 8,
            out_specs=vmem,
            scratch_shapes=[
                pltpu.VMEM((2, 2, height, SW, width), BF16),
                pltpu.VMEM((1, 2, height, SW, width), BF16),
                pltpu.VMEM((2, chunks, 8, SH * SW), jnp.int32),
                pltpu.VMEM((2, chunks, 8, SH * SW), jnp.int32),
                pltpu.VMEM((1, height), jnp.int32),
                pltpu.VMEM((breadth, height), jnp.int32),
                pltpu.VMEM(gains.shape, F32),
                pltpu.VMEM(w_in.shape, BF16),
                pltpu.VMEM(w_out.shape, BF16),
                pltpu.VMEM(w_up.shape, BF16),
                pltpu.VMEM(w_down.shape, BF16),
                pltpu.VMEM((count, 2 * pairs, 2 * cells, 128), BF16),
                pltpu.VMEM((count, 2 * pairs, 2 * cells, 128), BF16),
                pltpu.VMEM((count, 2 * pairs, 80, 2 * cells), BF16),
                pltpu.VMEM((count, 2, 2 * cells, 128), F32),
                pltpu.VMEM((count, 2 * pairs, 80, cells), F32),
                pltpu.VMEM((2 * count, width, cells), BF16),
                pltpu.SemaphoreType.DMA((pushes,)),
                pltpu.SemaphoreType.DMA((pushes,)),
                pltpu.SemaphoreType.DMA((12,)),
            ],
            compiler_params=pltpu.CompilerParams(
                collective_id=0, has_side_effects=True, vmem_limit_bytes=56 * 1024 * 1024
            ),
        )(atm, band[None, :], valid.T, gains, w_in, w_out, w_up, w_down)

    rows = P(("groups", "lat"), "lon", None)
    return jax.shard_map(
        on_device,
        mesh=mesh,
        in_specs=(rows, P(("groups", "lat")), P(("groups", "lat"), "lon"), P(), P(), P(), P(), P()),
        out_specs=rows,
        check_vma=False,
    )
```
